128 devices in a mesh: bx: 16 (over z, x), by: 8 (over y, core).
Axes of the slice: x: 4, y: 4, z: 4, core: 2. Of those that a mesh axis runs over, the one named last changes fastest.
Arguments:
- brick_ids: int32 [16384, 3], P(('bx', 'by')), may hold values from 0 to 255, all different within a row; in each aligned block of 128 rows (0 to 127, 128 to 255, ...) at most 5 rows name the same one
- cell_index: int32 [6, 3, 3, 16384], P(None, None, None, ('bx', 'by')), may hold values from 0 to 14
- cell_frac: float32 [6, 3, 3, 16384], P(None, None, None, ('bx', 'by')), may hold values from 0 to 1
- step_length: float32 [3, 3, 16384], P(None, None, ('bx', 'by')), may hold values from 0.01 to 0.05
- target: float32 [3, 16384], P(None, ('bx', 'by')), may hold values from 0 to 1
- planes: bfloat16 [256, 3, 256, 128], P(('bx', 'by')), may hold values from -6 to 6
- first_layer: bfloat16 [256, 128, 256], P(('bx', 'by')), may hold values from -0.5 to 0.5
- last_layer: bfloat16 [256, 4, 256], P(('bx', 'by')), may hold values from -0.375 to 0.375
Outputs:
- colour: float32 [3, 16384], P(None, ('bx', 'by'))
- plane_grad: float32 [256, 3, 256, 128], P(('bx', 'by'))
- first_grad: float32 [256, 128, 256], P(('bx', 'by'))
- last_grad: float32 [256, 4, 256], P(('bx', 'by'))
The draws below stay inside these ranges and needn't reach their ends.
Inputs may be any that keep to these rules, and one draw needn't show every extreme that they name: `brick_ids`: row r lists the 3 different bricks that ray r crosses, in the order in which it crosses them; among the rays of one device no brick is named more than 5 times.
All inputs are finite; a program needn't handle non-finite values.
Results may differ from the reference program's by a relative error of at most 0.007.
The reference program's roundings to bfloat16 on the way count: a program that leaves them out, or rounds other values in their place, can miss the bound.
Values sent between devices are 32-bit elements; how exact they have to be, the bound alone decides.
No kernel may reach another device: no remote copies, remote signals or barrier semaphores. Data moves between devices by JAX's collectives and lax.ppermute only.
A program may use at most 64 MiB of HBM per device.

```python
import math
import jax
import jax.numpy as jnp
import numpy as np
from jax import lax

RES = 16
CH = 128
HID = 256
SEG = 3
SAMP = 3
RAY_DEV = 128
BRICKS = 256
RAYS = 16384
CAP = 5
N_BX = 16
N_BY = 8


def touch_ends(array, key, least, top_value):
    index_at = [jax.random.randint(jax.random.fold_in(key, axis), (), 0, length) for axis, length in enumerate(array.shape)]
    main_axis = array.shape.index(max(array.shape))
    neighbour = index_at[:main_axis] + [(index_at[main_axis] + 1) % array.shape[main_axis]] + index_at[main_axis + 1:]
    return array.at[tuple(index_at)].set(least).at[tuple(neighbour)].set(top_value)


def shard_levels(key, dims, cuts, least, largest):
    gain, own = 1.0, jax.random.fold_in(key, 6)
    for axis_at, parts in cuts:
        heights = jnp.exp(jax.random.uniform(jax.random.fold_in(own, axis_at), (parts,), jnp.float32, least / len(cuts), largest / len(cuts)))
        gain = gain * jnp.repeat(heights, dims[axis_at] // parts).reshape([-1 if axis == axis_at else 1 for axis in range(len(dims))])
    return gain


def routed_block(own_key, own, number, rows, number_of, top, limit, lean):
    order = jax.random.permutation(own_key, number_of)
    heavy_load, common = portions_of(number_of, rows * top, limit, lean, True), portions_of(number_of, rows * top, limit, lean, False)
    places = jnp.arange(number_of)

    def named(lengths, offset_by):
        used = int((lengths > 0).sum())
        fixed = max(1, used // 4)
        passed = fixed + (places - fixed + offset_by * (used - fixed)) % max(1, number_of - fixed)
        return jnp.zeros((number_of,), jnp.int32).at[order[jnp.where(places < fixed, places, passed)]].set(jnp.asarray(lengths, jnp.int32))

    lengths = jnp.where(number % 4 == 0, named(heavy_load, number // 4), named(common, number - number // 4 - 1))
    mixed = jax.random.permutation(jax.random.fold_in(own, 3), number_of)
    source_of, receiver = mixed[0:number_of // 2 * 2:2], mixed[1:number_of // 2 * 2:2]
    room = jnp.minimum(lengths[source_of] - 1, limit - lengths[receiver]) // 2
    room = jnp.where((source_of == order[0]) | (receiver == order[0]) | (lengths[receiver] == 0), 0, jnp.maximum(room, 0))
    passed = jax.random.randint(jax.random.fold_in(own, 4), (number_of // 2,), 0, 1 << 20) % (room + 1)
    lengths = lengths.at[source_of].add(-passed).at[receiver].add(passed)
    labels = jnp.searchsorted(jnp.cumsum(lengths), jnp.arange(rows * top), side="right").astype(jnp.int32)
    listing = labels.reshape(top, rows).T
    listing = listing[jax.random.permutation(jax.random.fold_in(own, 1), rows)]
    offset_by = jax.random.randint(jax.random.fold_in(own, 2), (rows, 1), 0, top)
    return jnp.take_along_axis(listing, (jnp.arange(top)[None, :] + offset_by) % top, axis=1)


def portions_of(amount, total, limit, lean, full):
    weights = [(1 << 20) // math.isqrt(grade ** lean) + 1 for grade in range(1, amount + 1)]
    largest = limit if full else min(limit, max(-(-total // amount), total * weights[0] // sum(weights)))
    least = 1 if total - largest >= amount - 1 else 0
    counts, rest = [largest] + [least] * (amount - 1), total - largest - least * (amount - 1)
    while rest > 0:
        candidates = [i for i in range(1, amount) if counts[i] < largest] or [i for i in range(1, amount) if counts[i] < limit]
        mass, budget = sum([weights[i] for i in candidates]), rest
        for i in candidates:
            more = min(limit - counts[i], max(1, budget * weights[i] // mass), rest)
            counts[i] = counts[i] + more
            rest = rest - more
    return np.array(counts)


def bell_draw(rng, shape, width, reach, shards=(), kind=jnp.bfloat16):
    level = shard_levels(rng, shape, shards, -0.22, 0.18) if shards else 1.0
    result = jax.random.normal(rng, shape, jnp.float32) * width * level
    return jnp.minimum(jnp.maximum(result, -reach), reach).astype(kind)


def setup_inputs(seed: int = 0) -> dict:
    splits = jax.random.split(jax.random.key(seed), 9)
    brick_ids_keys = jax.random.split(jax.random.fold_in(splits[0], 1), RAYS // RAY_DEV)
    brick_ids_turns = jax.random.permutation(jax.random.fold_in(splits[0], 3), RAYS // RAY_DEV)
    brick_ids = jax.vmap(lambda own, number: routed_block(jax.random.fold_in(splits[0], 2), own, number, RAY_DEV, BRICKS, SEG, CAP, 2))(brick_ids_keys, brick_ids_turns).reshape((RAYS, SEG))
    cell_index = touch_ends(jax.random.randint(splits[1], (6, SEG, SAMP, RAYS), 0, RES - 1), jax.random.fold_in(splits[1], 1), 0, (RES - 1) - 1).astype(jnp.int32)
    cell_frac = jnp.clip(1.0 * jax.random.uniform(splits[2], (6, SEG, SAMP, RAYS), jnp.float32) ** shard_levels(splits[2], (6, SEG, SAMP, RAYS), ((3, 128),), -0.2, 0.2), 0.0, 1.0)
    step_length = jnp.clip(jnp.exp(math.log(0.05) - 1.609438 * jax.random.uniform(splits[3], (SEG, SAMP, RAYS), jnp.float32) ** shard_levels(splits[3], (SEG, SAMP, RAYS), ((2, 128),), -0.2, 0.2)), 0.01, 0.05)
    target = jnp.clip(1.0 * jax.random.uniform(splits[4], (3, RAYS), jnp.float32) ** shard_levels(splits[4], (3, RAYS), ((1, 128),), -0.2, 0.2), 0.0, 1.0)
    planes = bell_draw(splits[5], (BRICKS, 3, RES * RES, CH), 1.0, 6.0, ((0, 128),))
    first_layer = bell_draw(splits[6], (BRICKS, CH, HID), CH ** -0.5, 0.5, ((0, 128),))
    last_layer = bell_draw(splits[7], (BRICKS, 4, HID), HID ** -0.5, 0.375, ((0, 128),))
    return dict(brick_ids=brick_ids, cell_index=cell_index, cell_frac=cell_frac, step_length=step_length, target=target, planes=planes, first_layer=first_layer, last_layer=last_layer)


def render_rays(density, shade, step_length, target):
    ray_total = density.shape[-1]
    optical = (density * step_length).reshape(-1, ray_total)
    colours = shade.reshape(3, -1, ray_total)
    inclusive = jnp.cumsum(optical, axis=0)
    exclusive = jnp.concatenate([jnp.zeros_like(optical[:1]), inclusive[:-1]], axis=0)
    weight = jnp.exp(-exclusive) * (1.0 - jnp.exp(-optical))
    colour = jnp.sum(weight[None] * colours, axis=1)
    residual = colour - target
    shade_dot = jnp.sum(colours * residual[:, None, :], axis=0)
    contrib = weight * shade_dot
    reverse = jnp.cumsum(contrib[::-1], axis=0)[::-1]
    after = jnp.concatenate([reverse[1:], jnp.zeros_like(reverse[:1])], axis=0)
    density_grad = (jnp.exp(-inclusive) * shade_dot - after) * step_length.reshape(-1, ray_total)
    shade_grad = weight[None] * residual[:, None, :]
    return colour, jnp.concatenate([density_grad[None], shade_grad], axis=0)


def corners(cell_a, cell_b, coord_a, coord_b):
    corner_list = []
    for shift_a in (0, 1):
        for shift_b in (0, 1):
            index_a = cell_a + shift_a
            index_b = cell_b + shift_b
            weight_a = jnp.maximum(0.0, 1.0 - jnp.abs(coord_a - index_a.astype(coord_a.dtype)))
            weight_b = jnp.maximum(0.0, 1.0 - jnp.abs(coord_b - index_b.astype(coord_b.dtype)))
            rounded = lax.optimization_barrier((weight_a * weight_b).astype(jnp.bfloat16))
            corner_list.append(((index_a * RES + index_b).astype(jnp.int32), rounded.astype(coord_a.dtype)))
    return corner_list


def brick_state(plane_set, first_weight, last_weight, cell_rows, data_rows):
    plane_data = plane_set.astype(jnp.float32)
    feature = jnp.zeros((data_rows.shape[1], CH), jnp.float32)
    pieces = []
    for orient in range(3):
        for cell_flat, weight in corners(cell_rows[2 * orient], cell_rows[2 * orient + 1], data_rows[2 * orient], data_rows[2 * orient + 1]):
            feature = feature + weight[:, None] * plane_data[orient][cell_flat]
            pieces.append((orient, cell_flat, weight))
    feature = feature.astype(jnp.bfloat16)
    before_relu = jnp.dot(feature, first_weight, preferred_element_type=jnp.float32)
    hidden = jnp.maximum(before_relu, 0.0).astype(jnp.bfloat16)
    raw_out = jnp.dot(hidden, last_weight.T, preferred_element_type=jnp.float32)
    return pieces, feature, before_relu, hidden, raw_out


def reference(brick_ids, cell_index, cell_frac, step_length, target, planes, first_layer, last_layer):
    devices = N_BX * N_BY
    grouped = brick_ids.reshape(devices, RAY_DEV * SEG)
    member = (grouped[:, :, None] == jnp.arange(BRICKS, dtype=jnp.int32)[None, None, :]).astype(jnp.int32)
    ranking = jnp.sum((jnp.cumsum(member, axis=1) - member) * member, axis=2)
    source = jnp.arange(devices, dtype=jnp.int32)[:, None]
    slot_of = ((grouped * devices + source) * CAP + ranking).reshape(RAYS * SEG).astype(jnp.int32)
    slot_total = BRICKS * devices * CAP
    row_total = devices * CAP * SAMP
    coords = cell_index.astype(jnp.float32) + cell_frac
    payload = jnp.concatenate([coords, step_length[None]], axis=0)
    seg_data = payload.transpose(3, 1, 0, 2).reshape(RAYS * SEG, 7, SAMP)
    seg_cells = cell_index.transpose(3, 1, 0, 2).reshape(RAYS * SEG, 6, SAMP)
    slot_data = jnp.zeros((slot_total, 7, SAMP), jnp.float32).at[slot_of].set(seg_data)
    slot_cells = jnp.zeros((slot_total, 6, SAMP), jnp.int32).at[slot_of].set(seg_cells)
    brick_data = slot_data.reshape(BRICKS, devices * CAP, 7, SAMP).transpose(0, 2, 1, 3).reshape(BRICKS, 7, row_total)
    brick_cells = slot_cells.reshape(BRICKS, devices * CAP, 6, SAMP).transpose(0, 2, 1, 3).reshape(BRICKS, 6, row_total)

    def forward_one(inputs):
        plane_set, first_weight, last_weight, cell_rows, data_rows = inputs
        raw_out = brick_state(plane_set, first_weight, last_weight, cell_rows, data_rows)[4]
        return jnp.concatenate([jax.nn.softplus(raw_out[:, 0])[None], jax.nn.sigmoid(raw_out[:, 1:]).T], axis=0)

    results = lax.map(forward_one, (planes, first_layer, last_layer, brick_cells, brick_data))
    slot_results = results.reshape(BRICKS, 4, devices * CAP, SAMP).transpose(0, 2, 1, 3).reshape(slot_total, 4, SAMP)
    seg_results = slot_results[slot_of].reshape(RAYS, SEG, 4, SAMP).transpose(2, 1, 3, 0)
    colour, cotangent = render_rays(seg_results[0], seg_results[1:], step_length, target)
    seg_cot = cotangent.reshape(4, SEG, SAMP, RAYS).transpose(3, 1, 0, 2).reshape(RAYS * SEG, 4, SAMP)
    slot_cot = jnp.zeros((slot_total, 4, SAMP), jnp.float32).at[slot_of].set(seg_cot)
    brick_cot = slot_cot.reshape(BRICKS, devices * CAP, 4, SAMP).transpose(0, 2, 1, 3).reshape(BRICKS, 4, row_total)

    def backward_one(inputs):
        plane_set, first_weight, last_weight, cell_rows, data_rows, cot_rows = inputs
        pieces, feature, before_relu, hidden, raw_out = brick_state(plane_set, first_weight, last_weight, cell_rows, data_rows)
        shade = jax.nn.sigmoid(raw_out[:, 1:]).T
        raw_grad = jnp.concatenate([(cot_rows[0] * jax.nn.sigmoid(raw_out[:, 0]))[None], cot_rows[1:] * shade * (1.0 - shade)], axis=0).astype(jnp.bfloat16)
        last_part = jnp.dot(raw_grad, hidden, preferred_element_type=jnp.float32)
        hidden_grad = jnp.dot(raw_grad.T, last_weight, preferred_element_type=jnp.float32)
        pre_grad = jnp.where(before_relu > 0, hidden_grad, 0.0).astype(jnp.bfloat16)
        first_part = jnp.dot(feature.T, pre_grad, preferred_element_type=jnp.float32)
        feature_bf = lax.optimization_barrier(jnp.dot(pre_grad, first_weight.T, preferred_element_type=jnp.float32).astype(jnp.bfloat16))
        feature_grad = feature_bf.astype(jnp.float32)
        plane_part = jnp.zeros((3, RES * RES, CH), jnp.float32)
        for orient, cell_flat, weight in pieces:
            plane_part = plane_part.at[orient, cell_flat].add(weight[:, None] * feature_grad)
        return plane_part, first_part, last_part

    plane_grad, first_grad, last_grad = lax.map(backward_one, (planes, first_layer, last_layer, brick_cells, brick_data, brick_cot))
    return colour, plane_grad, first_grad, last_grad
```

```python
import math

import jax
import jax.numpy as jnp
from jax import lax
from jax.experimental import pallas as pl
from jax.experimental.pallas import tpu as pltpu
from jax.sharding import PartitionSpec as P

F32 = jnp.float32
BF16 = jnp.bfloat16
AXES = ("bx", "by")


def pieces_of(value):
    high = value.astype(BF16)
    rest = value - high.astype(F32)
    middle = rest.astype(BF16)
    low = (rest - middle.astype(F32)).astype(BF16)
    return high, middle, low


def dot_t(a, b):
    return lax.dot_general(a, b, (((1,), (1,)), ((), ())), preferred_element_type=F32)


def row_iota(shape):
    return lax.broadcasted_iota(jnp.int32, shape, 0)


def scatter_kernel(ids_ref, cell_ref, frac_ref, out_ref, route_ref, coord_ref, *, lb, cap, devices):
    crossed, rays = ids_ref.shape
    fields, _, samples, _ = cell_ref.shape
    bricks = lb * devices
    ids = [ids_ref[c : c + 1, :] for c in range(crossed)]
    brick_rows = row_iota((bricks, rays))
    member = [brick_rows == jnp.broadcast_to(i, (bricks, rays)) for i in ids]
    named = member[0].astype(F32)
    for c in range(1, crossed):
        named = named + member[c].astype(F32)
    earlier = row_iota((rays, rays)) < lax.broadcasted_iota(jnp.int32, (rays, rays), 1)
    before = jnp.dot(
        named.astype(BF16), earlier.astype(F32).astype(BF16), preferred_element_type=F32
    )
    coord_ref[...] = jnp.zeros(coord_ref.shape, F32)
    shift = lb.bit_length() - 1
    device_rows = row_iota((devices, rays))
    hots, slots = [], [[], [], []]
    span = fields * 4
    pad = out_ref.shape[1] - lb * cap * span
    for c in range(crossed):
        rank = jnp.sum(jnp.where(member[c], before, 0.0), axis=0, keepdims=True).astype(jnp.int32)
        device = lax.shift_right_logical(ids[c], shift)
        slot = (ids[c] & (lb - 1)) * cap + rank
        route_ref[c : c + 1, :] = device
        route_ref[4 + c : 5 + c, :] = slot
        hots.append((device_rows == jnp.broadcast_to(device, (devices, rays))).astype(F32).astype(BF16))
        for f in range(fields):
            coord_ref[c, f * 4 : f * 4 + samples, :] = cell_ref[f, c].astype(F32) + frac_ref[f, c]
        value = coord_ref[c]
        here = jnp.broadcast_to(slot, (span, rays))
        rows = [jnp.where(here == q, value, 0.0) for q in range(lb * cap)]
        if pad:
            rows.append(jnp.zeros((pad, rays), F32))
        for n, part in enumerate(pieces_of(jnp.concatenate(rows, axis=0))):
            slots[n].append(part)
    hot = jnp.concatenate(hots, axis=1)
    total = None
    for n in range(3):
        part = dot_t(hot, jnp.concatenate(slots[n], axis=1))
        total = part if total is None else total + part
    out_ref[...] = total


def hat(value, place):
    return jnp.maximum(0.0, 1.0 - jnp.abs(value - place))


def result_row(q, s, lb, cap):
    return q * 8 + s * 4 if s < 2 else lb * cap * 8 + q * 4


def forward_kernel(
    arrived_ref, planes_ref, first_ref, last_ref, out_ref, table_ref, feature_ref, hidden_ref,
    slope_ref, turned_ref, rows_ref, result_ref, *, lb, cap, samples
):
    cells = planes_ref.shape[2]
    side = math.isqrt(cells)
    lanes = arrived_ref.shape[0]
    brick = pl.program_id(0)
    span = 24
    orients = planes_ref.shape[1]

    @pl.when(brick == 0)
    def _():
        turned_ref[...] = arrived_ref[...].T
        result_ref[...] = jnp.zeros(result_ref.shape, F32)

    rows_ref[...] = turned_ref[pl.ds(pl.multiple_of(brick * (cap * span), 8), cap * span), :]
    place = row_iota((side, lanes)).astype(F32)
    for k in range(cap):
        for s in range(samples):
            block = (k * samples + s) * lanes
            for p in range(orients):
                at = k * span + 8 * p + s
                x = jnp.broadcast_to(rows_ref[at : at + 1, :], (side, lanes))
                y = jnp.broadcast_to(rows_ref[at + 4 : at + 5, :], (side, lanes))
                across = hat(y, place)
                for a in range(side):
                    table_ref[0, p * cells + a * side : p * cells + (a + 1) * side, block : block + lanes] = (
                        hat(x, float(a)) * across
                    ).astype(BF16)
    planes_t = planes_ref[0].reshape(orients * cells, -1).T
    feature = jnp.dot(planes_t, table_ref[0], preferred_element_type=F32).astype(BF16)
    feature_ref[0] = feature
    before = jnp.dot(first_ref[0].T, feature, preferred_element_type=F32)
    hidden = jnp.maximum(before, 0.0).astype(BF16)
    hidden_ref[0] = hidden
    raw = jnp.dot(last_ref[0], hidden, preferred_element_type=F32)
    gate = jax.nn.sigmoid(raw)
    is_density = row_iota(raw.shape) == 0
    result = jnp.where(is_density, jax.nn.softplus(raw), gate)
    slope_ref[0] = jnp.where(is_density, gate, gate * (1.0 - gate))
    for b in range(lb):

        @pl.when(brick == b)
        def _(b=b):
            for k in range(cap):
                for s in range(samples):
                    block = (k * samples + s) * lanes
                    row = result_row(b * cap + k, s, lb, cap)
                    result_ref[row : row + 4, :] = result[:, block : block + lanes]

    @pl.when(brick == lb - 1)
    def _():
        out_ref[...] = result_ref[...].T


def render_kernel(
    returned_ref, route_ref, step_ref, target_ref, colour_ref, out_ref, *, lb, cap
):
    devices = returned_ref.shape[0]
    crossed, samples, rays = step_ref.shape
    slots = lb * cap
    turned = returned_ref[...].T
    parts = pieces_of(turned)
    device_rows = row_iota((devices, rays))
    hots = [
        (device_rows == jnp.broadcast_to(route_ref[c : c + 1, :], (devices, rays))).astype(F32).astype(BF16)
        for c in range(crossed)
    ]
    hot = jnp.concatenate(hots, axis=1)
    fetched = None
    for part in parts:
        piece = jnp.dot(part, hot, preferred_element_type=F32)
        fetched = piece if fetched is None else fetched + piece
    parity = lax.shift_right_logical(row_iota((8, rays)), 2)
    picked = []
    for c in range(crossed):
        slot = jnp.broadcast_to(route_ref[4 + c : 5 + c, :], (8, rays))
        block = fetched[:, c * rays : (c + 1) * rays]
        two = jnp.zeros((8, rays), F32)
        for q in range(slots):
            two = two + jnp.where(slot == q, block[q * 8 : q * 8 + 8], 0.0)
        third = jnp.zeros((8, rays), F32)
        for h in range(slots // 2):
            at = slots * 8 + h * 8
            held = slot == parity + 2 * h
            third = third + jnp.where(held, block[at : at + 8], 0.0)
        third = third[0:4] + third[4:8]
        picked += [two[0:4], two[4:8], third]
    steps = [step_ref[c, s : s + 1, :] for c in range(crossed) for s in range(samples)]
    count = crossed * samples
    depth = [picked[i][0:1] * steps[i] for i in range(count)]
    inclusive, running = [], None
    for i in range(count):
        running = depth[i] if running is None else running + depth[i]
        inclusive.append(running)
    weight = []
    for i in range(count):
        through = 1.0 - jnp.exp(-depth[i])
        weight.append(through if i == 0 else jnp.exp(-inclusive[i - 1]) * through)
    colour = None
    for i in range(count):
        term = weight[i] * picked[i][1:4]
        colour = term if colour is None else colour + term
    colour_ref[...] = colour
    residual = colour - target_ref[...]
    dots = [jnp.sum(picked[i][1:4] * residual, axis=0, keepdims=True) for i in range(count)]
    after = [None] * count
    tail = jnp.zeros((1, rays), F32)
    for i in reversed(range(count)):
        after[i] = tail
        tail = tail + weight[i] * dots[i]
    cots = []
    for i in range(count):
        density_cot = (jnp.exp(-inclusive[i]) * dots[i] - after[i]) * steps[i]
        cots.append(jnp.concatenate([density_cot, weight[i] * residual], axis=0))
    placed = [[], [], []]
    for c in range(crossed):
        slot = jnp.broadcast_to(route_ref[4 + c : 5 + c, :], (8, rays))
        two = jnp.concatenate([cots[c * samples], cots[c * samples + 1]], axis=0)
        third = jnp.concatenate([cots[c * samples + 2]] * 2, axis=0)
        rows = [jnp.where(slot == q, two, 0.0) for q in range(slots)]
        for h in range(slots // 2):
            rows.append(jnp.where(slot == parity + 2 * h, third, 0.0))
        pad = out_ref.shape[1] - slots * 12
        if pad:
            rows.append(jnp.zeros((pad, rays), F32))
        for n, part in enumerate(pieces_of(jnp.concatenate(rows, axis=0))):
            placed[n].append(part)
    total = None
    for n in range(3):
        part = dot_t(hot, jnp.concatenate(placed[n], axis=1))
        total = part if total is None else total + part
    out_ref[...] = total


def backward_kernel(
    arrived_ref, table_ref, feature_ref, hidden_ref, slope_ref, first_ref, last_ref,
    plane_ref, first_grad_ref, last_grad_ref, turned_ref, cot_ref, *, lb, cap, samples
):
    lanes = arrived_ref.shape[0]
    brick = pl.program_id(0)

    @pl.when(brick == 0)
    def _():
        turned_ref[...] = arrived_ref[...].T

    for b in range(lb):

        @pl.when(brick == b)
        def _(b=b):
            for k in range(cap):
                for s in range(samples):
                    block = (k * samples + s) * lanes
                    row = result_row(b * cap + k, s, lb, cap)
                    cot_ref[:, block : block + lanes] = turned_ref[row : row + 4, :]

    raw_cot = (cot_ref[...] * slope_ref[0]).astype(BF16)
    hidden = hidden_ref[0]
    last_grad_ref[0] = dot_t(raw_cot, hidden)
    hidden_cot = jnp.dot(last_ref[0].astype(F32).T.astype(BF16), raw_cot, preferred_element_type=F32)
    before_cot = jnp.where(hidden.astype(F32) > 0, hidden_cot, 0.0).astype(BF16)
    first_grad_ref[0] = dot_t(feature_ref[0], before_cot)
    feature_cot = jnp.dot(first_ref[0], before_cot, preferred_element_type=F32).astype(BF16)
    orients, cells, channels = plane_ref.shape[1:]
    plane_ref[0] = dot_t(table_ref[0], feature_cot).reshape(orients, cells, channels)


def exchange(block):
    return lax.all_to_all(block, AXES, split_axis=0, concat_axis=0, tiled=True)


def whole(shape):
    return pl.BlockSpec(shape, lambda *_: (0,) * len(shape))


def per_brick(shape):
    return pl.BlockSpec((1,) + tuple(shape[1:]), lambda b: (b,) + (0,) * (len(shape) - 1))


def on_device(
    brick_ids, cell_index, cell_frac, step_length, target, planes, first_layer, last_layer
):
    devices = lax.axis_size("bx") * lax.axis_size("by")
    lb, orients, cells, channels = planes.shape
    rays, crossed = brick_ids.shape
    samples = step_length.shape[1]
    hidden_units = first_layer.shape[2]
    bricks = lb * devices
    cap = max(2, (3 * rays * crossed + bricks - 1) // bricks)
    fields = cell_index.shape[0]
    width = -(-lb * cap * fields * 4 // 128) * 128
    back = -(-lb * cap * 12 // 128) * 128
    rows = cap * samples * devices
    shape = jax.ShapeDtypeStruct

    outgoing, route = pl.pallas_call(
        lambda *refs: scatter_kernel(*refs, lb=lb, cap=cap, devices=devices),
        out_shape=(shape((devices, width), F32), shape((8, rays), jnp.int32)),
        scratch_shapes=[pltpu.VMEM((crossed, fields * 4, rays), F32)],
        name="scatter",
    )(brick_ids.T, cell_index, cell_frac)
    arrived = exchange(outgoing)

    saved = (
        shape((lb, orients * cells, rows), BF16),
        shape((lb, channels, rows), BF16),
        shape((lb, hidden_units, rows), BF16),
        shape((lb, 4, rows), F32),
    )
    results, table, feature, hidden, slope = pl.pallas_call(
        lambda *refs: forward_kernel(*refs, lb=lb, cap=cap, samples=samples),
        grid=(lb,),
        in_specs=[
            whole(arrived.shape), per_brick(planes.shape), per_brick(first_layer.shape),
            per_brick(last_layer.shape),
        ],
        out_specs=(whole((devices, back)),) + tuple(per_brick(s.shape) for s in saved),
        out_shape=(shape((devices, back), F32),) + saved,
        scratch_shapes=[
            pltpu.VMEM((width, devices), F32),
            pltpu.VMEM((cap * fields * 4, devices), F32),
            pltpu.VMEM((back, devices), F32),
        ],
        name="forward",
    )(arrived, planes, first_layer, last_layer)
    returned = exchange(results)

    colour, cot_out = pl.pallas_call(
        lambda *refs: render_kernel(*refs, lb=lb, cap=cap),
        out_shape=(shape(target.shape, F32), shape((devices, back), F32)),
        name="render",
    )(returned, route, step_length, target)
    cot_in = exchange(cot_out)

    grads = (
        shape(planes.shape, F32),
        shape(first_layer.shape, F32),
        shape(last_layer.shape, F32),
    )
    plane_grad, first_grad, last_grad = pl.pallas_call(
        lambda *refs: backward_kernel(*refs, lb=lb, cap=cap, samples=samples),
        grid=(lb,),
        in_specs=[whole(cot_in.shape)] + [per_brick(s.shape) for s in saved]
        + [per_brick(first_layer.shape), per_brick(last_layer.shape)],
        out_specs=tuple(per_brick(s.shape) for s in grads),
        out_shape=grads,
        scratch_shapes=[pltpu.VMEM((back, devices), F32), pltpu.VMEM((4, rows), F32)],
        name="backward",
    )(cot_in, table, feature, hidden, slope, first_layer, last_layer)
    return colour, plane_grad, first_grad, last_grad


def solution(mesh):
    return jax.shard_map(
        on_device,
        mesh=mesh,
        in_specs=(
            P(AXES, None),
            P(None, None, None, AXES),
            P(None, None, None, AXES),
            P(None, None, AXES),
            P(None, AXES),
            P(AXES, None, None, None),
            P(AXES, None, None),
            P(AXES, None, None),
        ),
        out_specs=(
            P(None, AXES),
            P(AXES, None, None, None),
            P(AXES, None, None),
            P(AXES, None, None),
        ),
        check_vma=False,
    )
```

```python
import math

import jax
import jax.numpy as jnp
from jax import lax
from jax.experimental import pallas as pl
from jax.experimental.pallas import tpu as pltpu
from jax.sharding import PartitionSpec as P

F32 = jnp.float32
BF16 = jnp.bfloat16
AXES = ("bx", "by")


def pieces_of(value):
    high = value.astype(BF16)
    rest = value - high.astype(F32)
    middle = rest.astype(BF16)
    low = (rest - middle.astype(F32)).astype(BF16)
    return high, middle, low


def dot_t(a, b):
    return lax.dot_general(a, b, (((1,), (1,)), ((), ())), preferred_element_type=F32)


def row_iota(shape):
    return lax.broadcasted_iota(jnp.int32, shape, 0)


def scatter_kernel(
    ids_in, cell_in, frac_in, *refs, lb, cap, devices
):
    carried = len(refs) // 2 - 3
    moved_in, (out_ref, route_ref), moved_out = refs[:carried], refs[carried : carried + 2], refs[carried + 2 : 2 * carried + 2]
    ids_ref, cell_ref, frac_ref, coord_ref, sems = refs[2 * carried + 2 :]
    sources = (ids_in, cell_in, frac_in) + tuple(moved_in)
    copies = [
        pltpu.make_async_copy(source, held, sems.at[n])
        for n, (source, held) in enumerate(zip(sources, (ids_ref, cell_ref, frac_ref) + tuple(moved_out)))
    ]
    for copy in copies:
        copy.start()
    copies[0].wait()
    crossed, rays = ids_ref.shape
    fields, _, samples, _ = cell_ref.shape
    bricks = lb * devices
    ids = [ids_ref[c : c + 1, :] for c in range(crossed)]
    brick_rows = row_iota((bricks, rays))
    member = [brick_rows == jnp.broadcast_to(i, (bricks, rays)) for i in ids]
    named = member[0].astype(F32)
    for c in range(1, crossed):
        named = named + member[c].astype(F32)
    earlier = row_iota((rays, rays)) < lax.broadcasted_iota(jnp.int32, (rays, rays), 1)
    before = jnp.dot(
        named.astype(BF16), earlier.astype(F32).astype(BF16), preferred_element_type=F32
    )
    coord_ref[...] = jnp.zeros(coord_ref.shape, F32)
    copies[1].wait()
    copies[2].wait()
    shift = lb.bit_length() - 1
    device_rows = row_iota((devices, rays))
    hots, slots = [], [[], [], []]
    span = fields * 4
    halves = out_ref.shape[0] // devices
    pad = halves * 128 - lb * cap * span
    for c in range(crossed):
        rank = jnp.sum(jnp.where(member[c], before, 0.0), axis=0, keepdims=True).astype(jnp.int32)
        device = lax.shift_right_logical(ids[c], shift)
        slot = (ids[c] & (lb - 1)) * cap + rank
        route_ref[c : c + 1, :] = device
        route_ref[4 + c : 5 + c, :] = slot
        hots.append((device_rows == jnp.broadcast_to(device, (devices, rays))).astype(F32).astype(BF16))
        for f in range(fields):
            coord_ref[c, f * 4 : f * 4 + samples, :] = cell_ref[f, c].astype(F32) + frac_ref[f, c]
        value = coord_ref[c]
        here = jnp.broadcast_to(slot, (span, rays))
        rows = [jnp.where(here == q, value, 0.0) for q in range(lb * cap)]
        if pad:
            rows.append(jnp.zeros((pad, rays), F32))
        for n, part in enumerate(pieces_of(jnp.concatenate(rows, axis=0))):
            slots[n].append(part)
    hot = jnp.concatenate(hots, axis=1)
    total = None
    for n in range(3):
        part = dot_t(hot, jnp.concatenate(slots[n], axis=1))
        total = part if total is None else total + part
    for h in range(halves):
        out_ref[pl.ds(h, devices, stride=halves), :] = total[:, h * 128 : h * 128 + 128]
    for copy in copies[3:]:
        copy.wait()


def hat(value, place):
    return jnp.maximum(0.0, 1.0 - jnp.abs(value - place))


def result_row(q, s, lb, cap):
    return q * 8 + s * 4 if s < 2 else lb * cap * 8 + q * 4


def forward_kernel(
    arrived_ref, planes_ref, first_ref, last_ref, out_ref, table_ref, feature_ref, hidden_ref,
    slope_ref, turned_ref, rows_ref, result_ref, *, lb, cap, samples, lanes
):
    orients, cells = planes_ref.shape[1:3]
    side = math.isqrt(cells)
    span = 24
    halves = arrived_ref.shape[0] // lanes
    for h in range(halves):
        turned_ref[h * 128 : h * 128 + 128, :] = arrived_ref[pl.ds(h, lanes, stride=halves), :].T
    result_ref[...] = jnp.zeros(result_ref.shape, F32)
    place = row_iota((side, lanes)).astype(F32)

    @pl.loop(0, lb)
    def _(brick):
        rows_ref[...] = turned_ref[pl.ds(pl.multiple_of(brick * (cap * span), 8), cap * span), :]
        for k in range(cap):
            for s in range(samples):
                block = (k * samples + s) * lanes
                for p in range(orients):
                    at = k * span + 8 * p + s
                    x = jnp.broadcast_to(rows_ref[at : at + 1, :], (side, lanes))
                    y = jnp.broadcast_to(rows_ref[at + 4 : at + 5, :], (side, lanes))
                    across = hat(y, place)
                    for a in range(side):
                        start = p * cells + a * side
                        table_ref[brick, start : start + side, block : block + lanes] = (
                            hat(x, float(a)) * across
                        ).astype(BF16)
        planes_t = planes_ref[brick].reshape(orients * cells, -1).T
        feature = jnp.dot(planes_t, table_ref[brick], preferred_element_type=F32).astype(BF16)
        feature_ref[brick] = feature
        before = jnp.dot(first_ref[brick].T, feature, preferred_element_type=F32)
        hidden = jnp.maximum(before, 0.0).astype(BF16)
        hidden_ref[brick] = hidden
        raw = jnp.dot(last_ref[brick], hidden, preferred_element_type=F32)
        gate = jax.nn.sigmoid(raw)
        is_density = row_iota(raw.shape) == 0
        result = jnp.where(is_density, jax.nn.softplus(raw), gate)
        slope_ref[brick] = jnp.where(is_density, gate, gate * (1.0 - gate))
        for b in range(lb):

            @pl.when(brick == b)
            def _(b=b):
                for k in range(cap):
                    for s in range(samples):
                        block = (k * samples + s) * lanes
                        row = result_row(b * cap + k, s, lb, cap)
                        result_ref[row : row + 4, :] = result[:, block : block + lanes]

    out_ref[...] = result_ref[...].T


def render_kernel(
    returned_ref, route_ref, step_ref, target_ref, colour_ref, out_ref, *, lb, cap
):
    devices = returned_ref.shape[0]
    crossed, samples, rays = step_ref.shape
    slots = lb * cap
    turned = returned_ref[...].T
    parts = pieces_of(turned)
    device_rows = row_iota((devices, rays))
    hots = [
        (device_rows == jnp.broadcast_to(route_ref[c : c + 1, :], (devices, rays))).astype(F32).astype(BF16)
        for c in range(crossed)
    ]
    hot = jnp.concatenate(hots, axis=1)
    fetched = None
    for part in parts:
        piece = jnp.dot(part, hot, preferred_element_type=F32)
        fetched = piece if fetched is None else fetched + piece
    parity = lax.shift_right_logical(row_iota((8, rays)), 2)
    picked = []
    for c in range(crossed):
        slot = jnp.broadcast_to(route_ref[4 + c : 5 + c, :], (8, rays))
        block = fetched[:, c * rays : (c + 1) * rays]
        two = jnp.zeros((8, rays), F32)
        for q in range(slots):
            two = two + jnp.where(slot == q, block[q * 8 : q * 8 + 8], 0.0)
        third = jnp.zeros((8, rays), F32)
        for h in range(slots // 2):
            at = slots * 8 + h * 8
            held = slot == parity + 2 * h
            third = third + jnp.where(held, block[at : at + 8], 0.0)
        third = third[0:4] + third[4:8]
        picked += [two[0:4], two[4:8], third]
    steps = [step_ref[c, s : s + 1, :] for c in range(crossed) for s in range(samples)]
    count = crossed * samples
    depth = [picked[i][0:1] * steps[i] for i in range(count)]
    inclusive, running = [], None
    for i in range(count):
        running = depth[i] if running is None else running + depth[i]
        inclusive.append(running)
    weight = []
    for i in range(count):
        through = 1.0 - jnp.exp(-depth[i])
        weight.append(through if i == 0 else jnp.exp(-inclusive[i - 1]) * through)
    colour = None
    for i in range(count):
        term = weight[i] * picked[i][1:4]
        colour = term if colour is None else colour + term
    colour_ref[...] = colour
    residual = colour - target_ref[...]
    dots = [jnp.sum(picked[i][1:4] * residual, axis=0, keepdims=True) for i in range(count)]
    after = [None] * count
    tail = jnp.zeros((1, rays), F32)
    for i in reversed(range(count)):
        after[i] = tail
        tail = tail + weight[i] * dots[i]
    cots = []
    for i in range(count):
        density_cot = (jnp.exp(-inclusive[i]) * dots[i] - after[i]) * steps[i]
        cots.append(jnp.concatenate([density_cot, weight[i] * residual], axis=0))
    placed = [[], [], []]
    for c in range(crossed):
        slot = jnp.broadcast_to(route_ref[4 + c : 5 + c, :], (8, rays))
        two = jnp.concatenate([cots[c * samples], cots[c * samples + 1]], axis=0)
        third = jnp.concatenate([cots[c * samples + 2]] * 2, axis=0)
        rows = [jnp.where(slot == q, two, 0.0) for q in range(slots)]
        for h in range(slots // 2):
            rows.append(jnp.where(slot == parity + 2 * h, third, 0.0))
        pad = out_ref.shape[1] - slots * 12
        if pad:
            rows.append(jnp.zeros((pad, rays), F32))
        for n, part in enumerate(pieces_of(jnp.concatenate(rows, axis=0))):
            placed[n].append(part)
    total = None
    for n in range(3):
        part = dot_t(hot, jnp.concatenate(placed[n], axis=1))
        total = part if total is None else total + part
    out_ref[...] = total


def backward_kernel(
    arrived_ref, table_ref, feature_ref, hidden_ref, slope_ref, first_ref, last_ref,
    plane_out, first_out, last_out, turned_ref, cot_ref, plane_ref, first_grad_ref, last_grad_ref,
    sems, *, lb, cap, samples
):
    lanes = arrived_ref.shape[0]
    turned_ref[...] = arrived_ref[...].T
    orients, cells, channels = plane_ref.shape[1:]
    pairs = ((plane_ref, plane_out), (first_grad_ref, first_out), (last_grad_ref, last_out))

    def copies(brick):
        return [
            pltpu.make_async_copy(held.at[brick], out.at[brick], sems.at[n, brick])
            for n, (held, out) in enumerate(pairs)
        ]

    @pl.loop(0, lb)
    def _(brick):
        for b in range(lb):

            @pl.when(brick == b)
            def _(b=b):
                for k in range(cap):
                    for s in range(samples):
                        block = (k * samples + s) * lanes
                        row = result_row(b * cap + k, s, lb, cap)
                        cot_ref[:, block : block + lanes] = turned_ref[row : row + 4, :]

        raw_cot = (cot_ref[...] * slope_ref[brick]).astype(BF16)
        hidden = hidden_ref[brick]
        last_grad_ref[brick] = dot_t(raw_cot, hidden)
        last_t = last_ref[brick].astype(F32).T.astype(BF16)
        hidden_cot = jnp.dot(last_t, raw_cot, preferred_element_type=F32)
        before_cot = jnp.where(hidden.astype(F32) > 0, hidden_cot, 0.0).astype(BF16)
        first_grad_ref[brick] = dot_t(feature_ref[brick], before_cot)
        feature_cot = jnp.dot(first_ref[brick], before_cot, preferred_element_type=F32).astype(BF16)
        plane_ref[brick] = dot_t(table_ref[brick], feature_cot).reshape(orients, cells, channels)
        for copy in copies(brick):
            copy.start()

    for b in range(lb):
        for copy in copies(b):
            copy.wait()


def exchange(block):
    return lax.all_to_all(block, AXES, split_axis=0, concat_axis=0, tiled=True)


def in_vmem(value):
    return pltpu.with_memory_space_constraint(value, pltpu.VMEM)


def params(mib):
    return pltpu.CompilerParams(vmem_limit_bytes=mib << 20)


def on_device(
    brick_ids, cell_index, cell_frac, step_length, target, planes, first_layer, last_layer
):
    devices = lax.axis_size("bx") * lax.axis_size("by")
    lb, orients, cells, channels = planes.shape
    rays, crossed = brick_ids.shape
    samples = step_length.shape[1]
    hidden_units = first_layer.shape[2]
    bricks = lb * devices
    cap = max(2, (3 * rays * crossed + bricks - 1) // bricks)
    fields = cell_index.shape[0]
    width = -(-lb * cap * fields * 4 // 128) * 128
    back = -(-lb * cap * 12 // 128) * 128
    rows = cap * samples * devices
    shape = jax.ShapeDtypeStruct

    moved = (planes, first_layer, last_layer, step_length, target)
    staged = (brick_ids.T, cell_index, cell_frac)
    outgoing, route, *moved = pl.pallas_call(
        lambda *refs: scatter_kernel(*refs, lb=lb, cap=cap, devices=devices),
        in_specs=[pl.BlockSpec(memory_space=pltpu.HBM)] * (len(staged) + len(moved)),
        out_shape=(pltpu.VMEM((devices * width // 128, 128), F32), pltpu.VMEM((8, rays), jnp.int32))
        + tuple(pltpu.VMEM(m.shape, m.dtype) for m in moved),
        scratch_shapes=[pltpu.VMEM(m.shape, m.dtype) for m in staged]
        + [
            pltpu.VMEM((crossed, fields * 4, rays), F32),
            pltpu.SemaphoreType.DMA((len(staged) + len(moved),)),
        ],
        compiler_params=params(8),
        name="scatter",
    )(*(pltpu.with_memory_space_constraint(m, pltpu.HBM) for m in staged + moved))
    planes, first_layer, last_layer, step_length, target = map(in_vmem, moved)
    arrived = exchange(outgoing)

    results, table, feature, hidden, slope = pl.pallas_call(
        lambda *refs: forward_kernel(*refs, lb=lb, cap=cap, samples=samples, lanes=devices),
        out_shape=(
            pltpu.VMEM((devices, back), F32),
            pltpu.VMEM((lb, orients * cells, rows), BF16),
            pltpu.VMEM((lb, channels, rows), BF16),
            pltpu.VMEM((lb, hidden_units, rows), BF16),
            pltpu.VMEM((lb, 4, rows), F32),
        ),
        scratch_shapes=[
            pltpu.VMEM((width, devices), F32),
            pltpu.VMEM((cap * fields * 4, devices), F32),
            pltpu.VMEM((back, devices), F32),
        ],
        compiler_params=params(24),
        name="forward",
    )(in_vmem(arrived), planes, first_layer, last_layer)
    returned = exchange(results)

    colour, cot_out = pl.pallas_call(
        lambda *refs: render_kernel(*refs, lb=lb, cap=cap),
        out_shape=(shape(target.shape, F32), pltpu.VMEM((devices, back), F32)),
        compiler_params=params(8),
        name="render",
    )(in_vmem(returned), in_vmem(route), step_length, target)
    cot_in = exchange(cot_out)

    grads = (
        shape((lb, orients, cells, channels), F32),
        shape((lb, channels, hidden_units), F32),
        shape((lb, 4, hidden_units), F32),
    )
    plane_grad, first_grad, last_grad = pl.pallas_call(
        lambda *refs: backward_kernel(*refs, lb=lb, cap=cap, samples=samples),
        out_specs=tuple(pl.BlockSpec(memory_space=pl.ANY) for _ in grads),
        out_shape=grads,
        scratch_shapes=[pltpu.VMEM((back, devices), F32), pltpu.VMEM((4, rows), F32)]
        + [pltpu.VMEM(g.shape, F32) for g in grads]
        + [pltpu.SemaphoreType.DMA((len(grads), lb))],
        compiler_params=params(24),
        name="backward",
    )(in_vmem(cot_in), *map(in_vmem, (table, feature, hidden, slope)), first_layer, last_layer)
    return colour, plane_grad, first_grad, last_grad


def solution(mesh):
    return jax.shard_map(
        on_device,
        mesh=mesh,
        in_specs=(
            P(AXES, None),
            P(None, None, None, AXES),
            P(None, None, None, AXES),
            P(None, None, AXES),
            P(None, AXES),
            P(AXES, None, None, None),
            P(AXES, None, None),
            P(AXES, None, None),
        ),
        out_specs=(
            P(None, AXES),
            P(AXES, None, None, None),
            P(AXES, None, None),
            P(AXES, None, None),
        ),
        check_vma=False,
    )
```

```python
import math

import jax
import jax.numpy as jnp
from jax import lax
from jax.experimental import pallas as pl
from jax.experimental.pallas import tpu as pltpu
from jax.sharding import PartitionSpec as P

F32 = jnp.float32
BF16 = jnp.bfloat16
AXES = ("bx", "by")
CHUNK = 15


def pieces_of(value):
    high = value.astype(BF16)
    rest = value - high.astype(F32)
    middle = rest.astype(BF16)
    low = (rest - middle.astype(F32)).astype(BF16)
    return high, middle, low


def dot_t(a, b):
    return lax.dot_general(a, b, (((1,), (1,)), ((), ())), preferred_element_type=F32)


def row_iota(shape):
    return lax.broadcasted_iota(jnp.int32, shape, 0)


def scatter_kernel(
    ids_in, cell_in, frac_in, *refs, lb, cap, devices
):
    carried = len(refs) // 2 - 3
    moved_in, (out_ref, route_ref), moved_out = refs[:carried], refs[carried : carried + 2], refs[carried + 2 : 2 * carried + 2]
    ids_ref, cell_ref, frac_ref, coord_ref, sems = refs[2 * carried + 2 :]
    sources = (ids_in, cell_in, frac_in) + tuple(moved_in)
    copies = [
        pltpu.make_async_copy(source, held, sems.at[n])
        for n, (source, held) in enumerate(zip(sources, (ids_ref, cell_ref, frac_ref) + tuple(moved_out)))
    ]
    for copy in copies:
        copy.start()
    copies[0].wait()
    crossed, rays = ids_ref.shape
    fields, _, samples, _ = cell_ref.shape
    bricks = lb * devices
    ids = [ids_ref[c : c + 1, :] for c in range(crossed)]
    brick_rows = row_iota((bricks, rays))
    member = [brick_rows == jnp.broadcast_to(i, (bricks, rays)) for i in ids]
    named = member[0].astype(F32)
    for c in range(1, crossed):
        named = named + member[c].astype(F32)
    earlier = row_iota((rays, rays)) < lax.broadcasted_iota(jnp.int32, (rays, rays), 1)
    before = jnp.dot(
        named.astype(BF16), earlier.astype(F32).astype(BF16), preferred_element_type=F32
    )
    coord_ref[...] = jnp.zeros(coord_ref.shape, F32)
    copies[1].wait()
    copies[2].wait()
    shift = lb.bit_length() - 1
    device_rows = row_iota((devices, rays))
    hots, slots = [], [[], [], []]
    span = fields * 4
    halves = out_ref.shape[0] // devices
    pad = halves * 128 - lb * cap * span
    for c in range(crossed):
        rank = jnp.sum(jnp.where(member[c], before, 0.0), axis=0, keepdims=True).astype(jnp.int32)
        device = lax.shift_right_logical(ids[c], shift)
        slot = (ids[c] & (lb - 1)) * 8 + rank
        route_ref[c : c + 1, :] = device
        route_ref[4 + c : 5 + c, :] = slot
        hots.append((device_rows == jnp.broadcast_to(device, (devices, rays))).astype(F32).astype(BF16))
        for f in range(fields):
            coord_ref[c, f * 4 : f * 4 + samples, :] = cell_ref[f, c].astype(F32) + frac_ref[f, c]
        value = coord_ref[c]
        here = jnp.broadcast_to(slot, (span, rays))
        rows = [jnp.where(here == b * 8 + k, value, 0.0) for b in range(lb) for k in range(cap)]
        if pad:
            rows.append(jnp.zeros((pad, rays), F32))
        for n, part in enumerate(pieces_of(jnp.concatenate(rows, axis=0))):
            slots[n].append(part)
    hot = jnp.concatenate(hots, axis=1)
    total = None
    for n in range(3):
        part = dot_t(hot, jnp.concatenate(slots[n], axis=1))
        total = part if total is None else total + part
    for h in range(halves):
        out_ref[pl.ds(h, devices, stride=halves), :] = total[:, h * 128 : h * 128 + 128]
    for copy in copies[3:]:
        copy.wait()


def hat(value, place):
    return jnp.maximum(0.0, 1.0 - jnp.abs(value - place))


def result_row(k, s, cap):
    return k * 8 + s * 4 if s < 2 else cap * 8 + k * 4


def chunks_of(blocks, size):
    return [(n, min(size, blocks - n)) for n in range(0, blocks, size)]


def forward_kernel(
    arrived_ref, planes_ref, first_ref, last_ref, out_ref, table_ref, feature_ref, hidden_ref,
    slope_ref, turned_ref, hat_ref, result_ref, *, lb, cap, samples, lanes
):
    orients, cells = planes_ref.shape[1:3]
    side = math.isqrt(cells)
    span = 24
    halves = arrived_ref.shape[0] // lanes
    for h in range(halves):
        turned_ref[h * 128 : h * 128 + 128, :] = arrived_ref[pl.ds(h, lanes, stride=halves), :].T
    result_ref[...] = jnp.zeros(result_ref.shape, F32)
    place = row_iota((side, lanes)).astype(F32)

    for brick in range(lb):
        planes_t = planes_ref[brick].reshape(orients * cells, -1).T
        first_t = first_ref[brick].T
        for begin, count in chunks_of(cap * samples, CHUNK):
            for n in range(begin, begin + count):
                k, s = divmod(n, samples)
                for p in range(orients):
                    at = (brick * cap + k) * span + 8 * p + s
                    hat_ref[brick, n, p] = hat(jnp.broadcast_to(turned_ref[at : at + 1, :], (side, lanes)), place)
                    across = hat(jnp.broadcast_to(turned_ref[at + 4 : at + 5, :], (side, lanes)), place)
                    for a in range(side):
                        start = p * cells + a * side
                        along = jnp.broadcast_to(hat_ref[brick, n, p, a : a + 1, :], (side, lanes))
                        table_ref[brick, start : start + side, n * lanes : (n + 1) * lanes] = (
                            along * across
                        ).astype(BF16)
            part = slice(begin * lanes, (begin + count) * lanes)
            feature = jnp.dot(planes_t, table_ref[brick, :, part], preferred_element_type=F32).astype(BF16)
            feature_ref[brick, :, part] = feature
            before = jnp.dot(first_t, feature, preferred_element_type=F32)
            hidden = jnp.maximum(before, 0.0).astype(BF16)
            hidden_ref[brick, :, part] = hidden
            raw = jnp.dot(last_ref[brick], hidden, preferred_element_type=F32)
            gate = jax.nn.sigmoid(raw)
            is_density = row_iota(raw.shape) == 0
            result = jnp.where(is_density, jax.nn.softplus(raw), gate)
            slope_ref[brick, :, part] = jnp.where(is_density, gate, gate * (1.0 - gate))
            for n in range(begin, begin + count):
                k, s = divmod(n, samples)
                row = result_row(k, s, cap)
                result_ref[brick, row : row + 4, :] = result[:, (n - begin) * lanes : (n - begin + 1) * lanes]

    out_ref[...] = result_ref[...].reshape(out_ref.shape[1], lanes).T


def render_kernel(
    returned_ref, route_ref, step_ref, target_ref, colour_ref, out_ref, *, lb, cap
):
    devices = returned_ref.shape[0]
    crossed, samples, rays = step_ref.shape
    turned = returned_ref[...].T
    parts = pieces_of(turned)
    device_rows = row_iota((devices, rays))
    hots = [
        (device_rows == jnp.broadcast_to(route_ref[c : c + 1, :], (devices, rays))).astype(F32).astype(BF16)
        for c in range(crossed)
    ]
    hot = jnp.concatenate(hots, axis=1)
    fetched = None
    for part in parts:
        piece = jnp.dot(part, hot, preferred_element_type=F32)
        fetched = piece if fetched is None else fetched + piece
    parity = lax.shift_right_logical(row_iota((8, rays)), 2)
    picked = []
    for c in range(crossed):
        slot = jnp.broadcast_to(route_ref[4 + c : 5 + c, :], (8, rays))
        block = fetched[:, c * rays : (c + 1) * rays]
        two = jnp.zeros((8, rays), F32)
        third = jnp.zeros((8, rays), F32)
        for b in range(lb):
            for k in range(cap):
                at = b * 64 + k * 8
                two = two + jnp.where(slot == b * 8 + k, block[at : at + 8], 0.0)
            for k in range(0, cap, 2):
                at = b * 64 + cap * 8 + k * 4
                third = third + jnp.where(slot == parity + (b * 8 + k), block[at : at + 8], 0.0)
        third = third[0:4] + third[4:8]
        picked += [two[0:4], two[4:8], third]
    steps = [step_ref[c, s : s + 1, :] for c in range(crossed) for s in range(samples)]
    count = crossed * samples
    depth = [picked[i][0:1] * steps[i] for i in range(count)]
    inclusive, running = [], None
    for i in range(count):
        running = depth[i] if running is None else running + depth[i]
        inclusive.append(running)
    weight = []
    for i in range(count):
        through = 1.0 - jnp.exp(-depth[i])
        weight.append(through if i == 0 else jnp.exp(-inclusive[i - 1]) * through)
    colour = None
    for i in range(count):
        term = weight[i] * picked[i][1:4]
        colour = term if colour is None else colour + term
    colour_ref[...] = colour
    residual = colour - target_ref[...]
    dots = [jnp.sum(picked[i][1:4] * residual, axis=0, keepdims=True) for i in range(count)]
    after = [None] * count
    tail = jnp.zeros((1, rays), F32)
    for i in reversed(range(count)):
        after[i] = tail
        tail = tail + weight[i] * dots[i]
    cots = []
    for i in range(count):
        density_cot = (jnp.exp(-inclusive[i]) * dots[i] - after[i]) * steps[i]
        cots.append(jnp.concatenate([density_cot, weight[i] * residual], axis=0))
    placed = [[], [], []]
    for c in range(crossed):
        slot = jnp.broadcast_to(route_ref[4 + c : 5 + c, :], (8, rays))
        two = jnp.concatenate([cots[c * samples], cots[c * samples + 1]], axis=0)
        third = jnp.concatenate([cots[c * samples + 2]] * 2, axis=0)
        rows = []
        for b in range(lb):
            rows += [jnp.where(slot == b * 8 + k, two, 0.0) for k in range(cap)]
            rows += [jnp.where(slot == parity + (b * 8 + k), third, 0.0) for k in range(0, cap, 2)]
        for n, part in enumerate(pieces_of(jnp.concatenate(rows, axis=0))):
            placed[n].append(part)
    total = None
    for n in range(3):
        part = dot_t(hot, jnp.concatenate(placed[n], axis=1))
        total = part if total is None else total + part
    out_ref[...] = total


def backward_kernel(
    arrived_ref, table_ref, feature_ref, hidden_ref, slope_ref, first_ref, last_ref,
    plane_out, first_out, last_out, turned_ref, raw_cot_ref, before_cot_ref, feature_cot_ref, plane_ref, first_grad_ref, last_grad_ref,
    sems, *, lb, cap, samples
):
    lanes = arrived_ref.shape[0]
    turned_ref[...] = arrived_ref[...].T.reshape(turned_ref.shape)
    orients, cells, channels = plane_ref.shape[1:]
    pairs = ((plane_ref, plane_out), (first_grad_ref, first_out), (last_grad_ref, last_out))

    copies = []

    def send(n, brick, *part):
        held, out = pairs[n]
        copies.append(
            pltpu.make_async_copy(held.at[(brick,) + part], out.at[(brick,) + part], sems.at[len(copies)])
        )
        copies[-1].start()

    def over_halves(a, b):
        half = -(-a.shape[1] // 512) * 256
        return dot_t(a[:, :half], b[:, :half]) + dot_t(a[:, half:], b[:, half:])

    for brick in range(lb):
        last_t = last_ref[brick].astype(F32).T.astype(BF16)
        for begin, count in chunks_of(cap * samples, CHUNK):
            part = slice(begin * lanes, (begin + count) * lanes)
            cots = []
            for n in range(begin, begin + count):
                k, s = divmod(n, samples)
                row = result_row(k, s, cap)
                cots.append(turned_ref[brick, row : row + 4, :])
            raw_cot = (jnp.concatenate(cots, axis=1) * slope_ref[brick, :, part]).astype(BF16)
            raw_cot_ref[brick, :, part] = raw_cot
            hidden_cot = jnp.dot(last_t, raw_cot, preferred_element_type=F32).astype(BF16)
            zero = jnp.zeros((), BF16)
            before_cot = jnp.where(hidden_ref[brick, :, part] > zero, hidden_cot, zero)
            before_cot_ref[brick, :, part] = before_cot
            feature_cot_ref[brick, :, part] = jnp.dot(
                first_ref[brick], before_cot, preferred_element_type=F32
            ).astype(BF16)
    for brick in range(lb):
        plane_ref[brick] = dot_t(table_ref[brick], feature_cot_ref[brick]).reshape(orients, cells, channels)
        send(0, brick)
        first_grad_ref[brick] = over_halves(feature_ref[brick], before_cot_ref[brick])
        send(1, brick)
        last_grad_ref[brick] = over_halves(raw_cot_ref[brick], hidden_ref[brick])
        send(2, brick)
    for copy in copies:
        copy.wait()


def exchange(block):
    return lax.all_to_all(block, AXES, split_axis=0, concat_axis=0, tiled=True)


def in_vmem(value):
    return pltpu.with_memory_space_constraint(value, pltpu.VMEM)


def params(mib):
    return pltpu.CompilerParams(vmem_limit_bytes=mib << 20)


def on_device(
    brick_ids, cell_index, cell_frac, step_length, target, planes, first_layer, last_layer
):
    devices = lax.axis_size("bx") * lax.axis_size("by")
    lb, orients, cells, channels = planes.shape
    rays, crossed = brick_ids.shape
    samples = step_length.shape[1]
    hidden_units = first_layer.shape[2]
    bricks = lb * devices
    cap = max(2, (3 * rays * crossed + bricks - 1) // bricks)
    fields = cell_index.shape[0]
    width = -(-lb * cap * fields * 4 // 128) * 128
    back = lb * 64
    rows = cap * samples * devices
    shape = jax.ShapeDtypeStruct

    moved = (planes, first_layer, last_layer, step_length, target)
    staged = (brick_ids.T, cell_index, cell_frac)
    outgoing, route, *moved = pl.pallas_call(
        lambda *refs: scatter_kernel(*refs, lb=lb, cap=cap, devices=devices),
        in_specs=[pl.BlockSpec(memory_space=pltpu.HBM)] * (len(staged) + len(moved)),
        out_shape=(pltpu.VMEM((devices * width // 128, 128), F32), pltpu.VMEM((8, rays), jnp.int32))
        + tuple(pltpu.VMEM(m.shape, m.dtype) for m in moved),
        scratch_shapes=[pltpu.VMEM(m.shape, m.dtype) for m in staged]
        + [
            pltpu.VMEM((crossed, fields * 4, rays), F32),
            pltpu.SemaphoreType.DMA((len(staged) + len(moved),)),
        ],
        compiler_params=params(8),
        name="scatter",
    )(*(pltpu.with_memory_space_constraint(m, pltpu.HBM) for m in staged + moved))
    planes, first_layer, last_layer, step_length, target = map(in_vmem, moved)
    arrived = exchange(outgoing)

    results, table, feature, hidden, slope = pl.pallas_call(
        lambda *refs: forward_kernel(*refs, lb=lb, cap=cap, samples=samples, lanes=devices),
        out_shape=(
            pltpu.VMEM((devices, back), F32),
            pltpu.VMEM((lb, orients * cells, rows), BF16),
            pltpu.VMEM((lb, channels, rows), BF16),
            pltpu.VMEM((lb, hidden_units, rows), BF16),
            pltpu.VMEM((lb, 4, rows), F32),
        ),
        scratch_shapes=[
            pltpu.VMEM((width, devices), F32),
            pltpu.VMEM((lb, cap * samples, orients, math.isqrt(cells), devices), F32),
            pltpu.VMEM((lb, 64, devices), F32),
        ],
        compiler_params=params(24),
        name="forward",
    )(in_vmem(arrived), planes, first_layer, last_layer)
    returned = exchange(results)

    colour, cot_out = pl.pallas_call(
        lambda *refs: render_kernel(*refs, lb=lb, cap=cap),
        out_shape=(shape(target.shape, F32), pltpu.VMEM((devices, back), F32)),
        compiler_params=params(8),
        name="render",
    )(in_vmem(returned), in_vmem(route), step_length, target)
    cot_in = exchange(cot_out)

    grads = (
        shape((lb, orients, cells, channels), F32),
        shape((lb, channels, hidden_units), F32),
        shape((lb, 4, hidden_units), F32),
    )
    plane_grad, first_grad, last_grad = pl.pallas_call(
        lambda *refs: backward_kernel(*refs, lb=lb, cap=cap, samples=samples),
        out_specs=tuple(pl.BlockSpec(memory_space=pl.ANY) for _ in grads),
        out_shape=grads,
        scratch_shapes=[
            pltpu.VMEM((lb, 64, devices), F32),
            pltpu.VMEM((lb, 4, rows), BF16),
            pltpu.VMEM((lb, hidden_units, rows), BF16),
            pltpu.VMEM((lb, channels, rows), BF16),
        ]
        + [pltpu.VMEM(g.shape, F32) for g in grads]
        + [pltpu.SemaphoreType.DMA((len(grads) * lb,))],
        compiler_params=params(24),
        name="backward",
    )(in_vmem(cot_in), *map(in_vmem, (table, feature, hidden, slope)), first_layer, last_layer)
    return colour, plane_grad, first_grad, last_grad


def solution(mesh):
    return jax.shard_map(
        on_device,
        mesh=mesh,
        in_specs=(
            P(AXES, None),
            P(None, None, None, AXES),
            P(None, None, None, AXES),
            P(None, None, AXES),
            P(None, AXES),
            P(AXES, None, None, None),
            P(AXES, None, None),
            P(AXES, None, None),
        ),
        out_specs=(
            P(None, AXES),
            P(AXES, None, None, None),
            P(AXES, None, None),
            P(AXES, None, None),
        ),
        check_vma=False,
    )
```

```python
import math

import jax
import jax.numpy as jnp
from jax import lax
from jax.experimental import pallas as pl
from jax.experimental.pallas import tpu as pltpu
from jax.sharding import PartitionSpec as P

F32 = jnp.float32
BF16 = jnp.bfloat16
AXES = ("bx", "by")
CHUNK = 15


def pieces_of(value):
    high = value.astype(BF16)
    rest = value - high.astype(F32)
    middle = rest.astype(BF16)
    low = (rest - middle.astype(F32)).astype(BF16)
    return high, middle, low


def dot_t(a, b):
    return lax.dot_general(a, b, (((1,), (1,)), ((), ())), preferred_element_type=F32)


def row_iota(shape):
    return lax.broadcasted_iota(jnp.int32, shape, 0)


def scatter_kernel(
    ids_in, cell_in, frac_in, *refs, lb, cap, devices
):
    carried = len(refs) // 2 - 3
    moved_in, (out_ref, route_ref), moved_out = refs[:carried], refs[carried : carried + 2], refs[carried + 2 : 2 * carried + 2]
    ids_ref, cell_ref, frac_ref, coord_ref, sems = refs[2 * carried + 2 :]
    sources = (ids_in, cell_in, frac_in) + tuple(moved_in)
    copies = [
        pltpu.make_async_copy(source, held, sems.at[n])
        for n, (source, held) in enumerate(zip(sources, (ids_ref, cell_ref, frac_ref) + tuple(moved_out)))
    ]
    for copy in copies:
        copy.start()
    crossed, rays = ids_ref.shape
    fields, _, samples, _ = cell_ref.shape
    bricks = lb * devices
    earlier = row_iota((rays, rays)) < lax.broadcasted_iota(jnp.int32, (rays, rays), 1)
    earlier = earlier.astype(F32).astype(BF16)
    coord_ref[...] = jnp.zeros(coord_ref.shape, F32)
    copies[0].wait()
    ids = [ids_ref[c : c + 1, :] for c in range(crossed)]
    brick_rows = row_iota((bricks, rays))
    member = [brick_rows == jnp.broadcast_to(i, (bricks, rays)) for i in ids]
    named = member[0].astype(F32)
    for c in range(1, crossed):
        named = named + member[c].astype(F32)
    before = jnp.dot(named.astype(BF16), earlier, preferred_element_type=F32)
    copies[1].wait()
    copies[2].wait()
    shift = lb.bit_length() - 1
    device_rows = row_iota((devices, rays))
    hots, slots = [], [[], [], []]
    span = fields * 4
    halves = out_ref.shape[0] // devices
    pad = halves * 128 - lb * cap * span
    for c in range(crossed):
        rank = jnp.sum(jnp.where(member[c], before, 0.0), axis=0, keepdims=True).astype(jnp.int32)
        device = lax.shift_right_logical(ids[c], shift)
        slot = (ids[c] & (lb - 1)) * 8 + rank
        route_ref[c : c + 1, :] = device
        route_ref[4 + c : 5 + c, :] = slot
        hots.append((device_rows == jnp.broadcast_to(device, (devices, rays))).astype(F32).astype(BF16))
        for f in range(fields):
            coord_ref[c, f * 4 : f * 4 + samples, :] = cell_ref[f, c].astype(F32) + frac_ref[f, c]
        value = coord_ref[c]
        here = jnp.broadcast_to(slot, (span, rays))
        rows = [jnp.where(here == b * 8 + k, value, 0.0) for b in range(lb) for k in range(cap)]
        if pad:
            rows.append(jnp.zeros((pad, rays), F32))
        for n, part in enumerate(pieces_of(jnp.concatenate(rows, axis=0))):
            slots[n].append(part)
    hot = jnp.concatenate(hots, axis=1)
    total = None
    for n in range(3):
        part = dot_t(hot, jnp.concatenate(slots[n], axis=1))
        total = part if total is None else total + part
    for h in range(halves):
        out_ref[pl.ds(h, devices, stride=halves), :] = total[:, h * 128 : h * 128 + 128]
    for copy in copies[3:]:
        copy.wait()


def hat(value, place):
    return jnp.maximum(0.0, 1.0 - jnp.abs(value - place))


def result_row(k, s, cap):
    return k * 8 + s * 4 if s < 2 else cap * 8 + k * 4


def chunks_of(blocks, size):
    return [(n, min(size, blocks - n)) for n in range(0, blocks, size)]


def forward_kernel(
    arrived_ref, planes_ref, first_ref, last_ref, out_ref, table_ref, feature_ref, hidden_ref,
    slope_ref, turned_ref, hat_ref, result_ref, *, lb, cap, samples, lanes
):
    orients, cells = planes_ref.shape[1:3]
    side = math.isqrt(cells)
    span = 24
    halves = arrived_ref.shape[0] // lanes
    for h in range(halves):
        turned_ref[h * 128 : h * 128 + 128, :] = arrived_ref[pl.ds(h, lanes, stride=halves), :].T
    result_ref[...] = jnp.zeros(result_ref.shape, F32)
    place = row_iota((side, lanes)).astype(F32)

    for brick in range(lb):
        planes_t = planes_ref[brick].reshape(orients * cells, -1).T
        first_t = first_ref[brick].T
        for begin, count in chunks_of(cap * samples, CHUNK):
            for n in range(begin, begin + count):
                k, s = divmod(n, samples)
                for p in range(orients):
                    at = (brick * cap + k) * span + 8 * p + s
                    hat_ref[brick, n, p] = hat(jnp.broadcast_to(turned_ref[at : at + 1, :], (side, lanes)), place)
                    across = hat(jnp.broadcast_to(turned_ref[at + 4 : at + 5, :], (side, lanes)), place)
                    for a in range(side):
                        start = p * cells + a * side
                        along = jnp.broadcast_to(hat_ref[brick, n, p, a : a + 1, :], (side, lanes))
                        table_ref[brick, start : start + side, n * lanes : (n + 1) * lanes] = (
                            along * across
                        ).astype(BF16)
            part = slice(begin * lanes, (begin + count) * lanes)
            feature = jnp.dot(planes_t, table_ref[brick, :, part], preferred_element_type=F32).astype(BF16)
            feature_ref[brick, :, part] = feature
            before = jnp.dot(first_t, feature, preferred_element_type=F32)
            hidden = jnp.maximum(before, 0.0).astype(BF16)
            hidden_ref[brick, :, part] = hidden
            raw = jnp.dot(last_ref[brick], hidden, preferred_element_type=F32)
            gate = jax.nn.sigmoid(raw)
            is_density = row_iota(raw.shape) == 0
            result = jnp.where(is_density, jax.nn.softplus(raw), gate)
            slope_ref[brick, :, part] = jnp.where(is_density, gate, gate * (1.0 - gate))
            for n in range(begin, begin + count):
                k, s = divmod(n, samples)
                row = result_row(k, s, cap)
                result_ref[brick, row : row + 4, :] = result[:, (n - begin) * lanes : (n - begin + 1) * lanes]

    out_ref[...] = result_ref[...].reshape(out_ref.shape[1], lanes).T


def render_kernel(
    returned_ref, route_ref, step_ref, target_ref, colour_ref, out_ref, *, lb, cap
):
    devices = returned_ref.shape[0]
    crossed, samples, rays = step_ref.shape
    turned = returned_ref[...].T
    parts = pieces_of(turned)
    device_rows = row_iota((devices, rays))
    hots = [
        (device_rows == jnp.broadcast_to(route_ref[c : c + 1, :], (devices, rays))).astype(F32).astype(BF16)
        for c in range(crossed)
    ]
    hot = jnp.concatenate(hots, axis=1)
    fetched = None
    for part in parts:
        piece = jnp.dot(part, hot, preferred_element_type=F32)
        fetched = piece if fetched is None else fetched + piece
    parity = lax.shift_right_logical(row_iota((8, rays)), 2)
    picked = []
    for c in range(crossed):
        slot = jnp.broadcast_to(route_ref[4 + c : 5 + c, :], (8, rays))
        block = fetched[:, c * rays : (c + 1) * rays]
        two = jnp.zeros((8, rays), F32)
        third = jnp.zeros((8, rays), F32)
        for b in range(lb):
            for k in range(cap):
                at = b * 64 + k * 8
                two = two + jnp.where(slot == b * 8 + k, block[at : at + 8], 0.0)
            for k in range(0, cap, 2):
                at = b * 64 + cap * 8 + k * 4
                third = third + jnp.where(slot == parity + (b * 8 + k), block[at : at + 8], 0.0)
        third = third[0:4] + third[4:8]
        picked += [two[0:4], two[4:8], third]
    steps = [step_ref[c, s : s + 1, :] for c in range(crossed) for s in range(samples)]
    count = crossed * samples
    depth = [picked[i][0:1] * steps[i] for i in range(count)]
    inclusive, running = [], None
    for i in range(count):
        running = depth[i] if running is None else running + depth[i]
        inclusive.append(running)
    weight = []
    for i in range(count):
        through = 1.0 - jnp.exp(-depth[i])
        weight.append(through if i == 0 else jnp.exp(-inclusive[i - 1]) * through)
    colour = None
    for i in range(count):
        term = weight[i] * picked[i][1:4]
        colour = term if colour is None else colour + term
    colour_ref[...] = colour
    residual = colour - target_ref[...]
    dots = [jnp.sum(picked[i][1:4] * residual, axis=0, keepdims=True) for i in range(count)]
    after = [None] * count
    tail = jnp.zeros((1, rays), F32)
    for i in reversed(range(count)):
        after[i] = tail
        tail = tail + weight[i] * dots[i]
    cots = []
    for i in range(count):
        density_cot = (jnp.exp(-inclusive[i]) * dots[i] - after[i]) * steps[i]
        cots.append(jnp.concatenate([density_cot, weight[i] * residual], axis=0))
    placed = [[], [], []]
    for c in range(crossed):
        slot = jnp.broadcast_to(route_ref[4 + c : 5 + c, :], (8, rays))
        two = jnp.concatenate([cots[c * samples], cots[c * samples + 1]], axis=0)
        third = jnp.concatenate([cots[c * samples + 2]] * 2, axis=0)
        rows = []
        for b in range(lb):
            rows += [jnp.where(slot == b * 8 + k, two, 0.0) for k in range(cap)]
            rows += [jnp.where(slot == parity + (b * 8 + k), third, 0.0) for k in range(0, cap, 2)]
        for n, part in enumerate(pieces_of(jnp.concatenate(rows, axis=0))):
            placed[n].append(part)
    total = None
    for n in range(3):
        part = dot_t(hot, jnp.concatenate(placed[n], axis=1))
        total = part if total is None else total + part
    out_ref[...] = total


def backward_kernel(
    arrived_ref, colour_ref, table_ref, feature_ref, hidden_ref, slope_ref, first_ref, last_ref,
    colour_out, plane_out, first_out, last_out, turned_ref, raw_cot_ref, before_cot_ref, feature_cot_ref, plane_ref, first_grad_ref, last_grad_ref,
    sems, *, lb, cap, samples
):
    lanes = arrived_ref.shape[0]
    copies = [pltpu.make_async_copy(colour_ref, colour_out, sems.at[0])]
    copies[0].start()
    turned_ref[...] = arrived_ref[...].T.reshape(turned_ref.shape)
    orients, cells, channels = plane_ref.shape[1:]
    pairs = ((plane_ref, plane_out), (first_grad_ref, first_out), (last_grad_ref, last_out))

    def send(n, brick, *part):
        held, out = pairs[n]
        copies.append(
            pltpu.make_async_copy(held.at[(brick,) + part], out.at[(brick,) + part], sems.at[len(copies)])
        )
        copies[-1].start()

    def over_halves(a, b):
        half = -(-a.shape[1] // 512) * 256
        return dot_t(a[:, :half], b[:, :half]) + dot_t(a[:, half:], b[:, half:])

    for brick in range(lb):
        last_t = last_ref[brick].astype(F32).T.astype(BF16)
        for begin, count in chunks_of(cap * samples, CHUNK):
            part = slice(begin * lanes, (begin + count) * lanes)
            cots = []
            for n in range(begin, begin + count):
                k, s = divmod(n, samples)
                row = result_row(k, s, cap)
                cots.append(turned_ref[brick, row : row + 4, :])
            raw_cot = (jnp.concatenate(cots, axis=1) * slope_ref[brick, :, part]).astype(BF16)
            raw_cot_ref[brick, :, part] = raw_cot
            hidden_cot = jnp.dot(last_t, raw_cot, preferred_element_type=F32).astype(BF16)
            zero = jnp.zeros((), BF16)
            before_cot = jnp.where(hidden_ref[brick, :, part] > zero, hidden_cot, zero)
            before_cot_ref[brick, :, part] = before_cot
            feature_cot_ref[brick, :, part] = jnp.dot(
                first_ref[brick], before_cot, preferred_element_type=F32
            ).astype(BF16)
    for brick in range(lb):
        plane_ref[brick] = dot_t(table_ref[brick], feature_cot_ref[brick]).reshape(orients, cells, channels)
        send(0, brick)
        first_grad_ref[brick] = over_halves(feature_ref[brick], before_cot_ref[brick])
        send(1, brick)
        last_grad_ref[brick] = over_halves(raw_cot_ref[brick], hidden_ref[brick])
        send(2, brick)
    for copy in copies:
        copy.wait()


def exchange(block):
    return lax.all_to_all(block, AXES, split_axis=0, concat_axis=0, tiled=True)


def in_vmem(value):
    return pltpu.with_memory_space_constraint(value, pltpu.VMEM)


def params(mib):
    return pltpu.CompilerParams(vmem_limit_bytes=mib << 20)


def on_device(
    brick_ids, cell_index, cell_frac, step_length, target, planes, first_layer, last_layer
):
    devices = lax.axis_size("bx") * lax.axis_size("by")
    lb, orients, cells, channels = planes.shape
    rays, crossed = brick_ids.shape
    samples = step_length.shape[1]
    hidden_units = first_layer.shape[2]
    bricks = lb * devices
    cap = max(2, (3 * rays * crossed + bricks - 1) // bricks)
    fields = cell_index.shape[0]
    width = -(-lb * cap * fields * 4 // 128) * 128
    back = lb * 64
    rows = cap * samples * devices
    shape = jax.ShapeDtypeStruct

    moved = (planes, first_layer, last_layer, step_length, target)
    staged = (brick_ids.T, cell_index, cell_frac)
    outgoing, route, *moved = pl.pallas_call(
        lambda *refs: scatter_kernel(*refs, lb=lb, cap=cap, devices=devices),
        in_specs=[pl.BlockSpec(memory_space=pltpu.HBM)] * (len(staged) + len(moved)),
        out_shape=(pltpu.VMEM((devices * width // 128, 128), F32), pltpu.VMEM((8, rays), jnp.int32))
        + tuple(pltpu.VMEM(m.shape, m.dtype) for m in moved),
        scratch_shapes=[pltpu.VMEM(m.shape, m.dtype) for m in staged]
        + [
            pltpu.VMEM((crossed, fields * 4, rays), F32),
            pltpu.SemaphoreType.DMA((len(staged) + len(moved),)),
        ],
        compiler_params=params(8),
        name="scatter",
    )(*(pltpu.with_memory_space_constraint(m, pltpu.HBM) for m in staged + moved))
    planes, first_layer, last_layer, step_length, target = map(in_vmem, moved)
    arrived = exchange(outgoing)

    results, table, feature, hidden, slope = pl.pallas_call(
        lambda *refs: forward_kernel(*refs, lb=lb, cap=cap, samples=samples, lanes=devices),
        out_shape=(
            pltpu.VMEM((devices, back), F32),
            pltpu.VMEM((lb, orients * cells, rows), BF16),
            pltpu.VMEM((lb, channels, rows), BF16),
            pltpu.VMEM((lb, hidden_units, rows), BF16),
            pltpu.VMEM((lb, 4, rows), F32),
        ),
        scratch_shapes=[
            pltpu.VMEM((width, devices), F32),
            pltpu.VMEM((lb, cap * samples, orients, math.isqrt(cells), devices), F32),
            pltpu.VMEM((lb, 64, devices), F32),
        ],
        compiler_params=params(24),
        name="forward",
    )(in_vmem(arrived), planes, first_layer, last_layer)
    returned = exchange(results)

    colour, cot_out = pl.pallas_call(
        lambda *refs: render_kernel(*refs, lb=lb, cap=cap),
        out_shape=(pltpu.VMEM(target.shape, F32), pltpu.VMEM((devices, back), F32)),
        compiler_params=params(8),
        name="render",
    )(in_vmem(returned), in_vmem(route), step_length, target)
    cot_in = exchange(cot_out)

    grads = (
        shape(target.shape, F32),
        shape((lb, orients, cells, channels), F32),
        shape((lb, channels, hidden_units), F32),
        shape((lb, 4, hidden_units), F32),
    )
    return pl.pallas_call(
        lambda *refs: backward_kernel(*refs, lb=lb, cap=cap, samples=samples),
        out_specs=tuple(pl.BlockSpec(memory_space=pl.ANY) for _ in grads),
        out_shape=grads,
        scratch_shapes=[
            pltpu.VMEM((lb, 64, devices), F32),
            pltpu.VMEM((lb, 4, rows), BF16),
            pltpu.VMEM((lb, hidden_units, rows), BF16),
            pltpu.VMEM((lb, channels, rows), BF16),
        ]
        + [pltpu.VMEM(g.shape, F32) for g in grads[1:]]
        + [pltpu.SemaphoreType.DMA((1 + 3 * lb,))],
        compiler_params=params(24),
        name="backward",
    )(*map(in_vmem, (cot_in, colour, table, feature, hidden, slope)), first_layer, last_layer)


def solution(mesh):
    return jax.shard_map(
        on_device,
        mesh=mesh,
        in_specs=(
            P(AXES, None),
            P(None, None, None, AXES),
            P(None, None, None, AXES),
            P(None, None, AXES),
            P(None, AXES),
            P(AXES, None, None, None),
            P(AXES, None, None),
            P(AXES, None, None),
        ),
        out_specs=(
            P(None, AXES),
            P(AXES, None, None, None),
            P(AXES, None, None),
            P(AXES, None, None),
        ),
        check_vma=False,
    )
```
